32 devices in a mesh: dp: 2 (over y), ctx: 4 (over z), fsdp: 4 (over x, core).
Axes of the slice: x: 2, y: 2, z: 4, core: 2. Of those that a mesh axis runs over, the one named last changes fastest.
Arguments:
- grad_parts: bfloat16 [2, 2, 512, 16384], P('dp', None, 'fsdp', 'ctx'), may hold values from -6 to 6
- weight: bfloat16 [2, 512, 16384], P('dp', 'fsdp', 'ctx'), may hold values from -0.25 to 0.25
- logit_max: float32 [2, 4, 2, 64], P('dp', 'ctx'), may hold values from 10 to 1000
Outputs:
- update: float32 [2, 512, 16384], P('dp', 'fsdp', 'ctx')
- new_weight: float32 [2, 512, 16384], P('dp', 'fsdp', 'ctx')
The draws below stay inside these ranges and needn't reach their ends.
All inputs are finite; a program needn't handle non-finite values.
Results may differ from the reference program's by a relative error of at most 0.0003.
Values sent between devices are 32-bit elements; how exact they have to be, the bound alone decides.
A program may use at most 64 MiB of HBM per device.

```python
import math
import jax
import jax.numpy as jnp
from jax import lax

KV_RANK = 512
HEADS = 64
NOPE = 128
V_DIM = 128
ITERS = 2
LAYERS = 2
COLS = 16384
N_DP = 2
N_CTX = 4


def with_spikes(result, key, source, target, parts, factor):
    owner, partner = [(jnp.arange(result.shape[dim]) // (result.shape[dim] // parts)).reshape([-1 if axis == dim else 1 for axis in range(result.ndim)]) for dim in (source, target)]
    chosen = jax.random.permutation(key, parts)[partner]
    strong = (owner == chosen) | (owner == (partner + parts // 2) % parts)
    return jnp.where(strong, factor * result, result)


def level_of(own_key, shape, split, least, largest):
    def one(position, shards_of):
        steps = jax.random.uniform(jax.random.fold_in(jax.random.fold_in(own_key, 6), position), (shards_of,), jnp.float32, least / len(split), largest / len(split))
        return jnp.repeat(jnp.exp(steps), shape[position] // shards_of).reshape((-1,) + (1,) * (len(shape) - position - 1))

    loudness = one(*split[0])
    for cut in split[1:]:
        loudness = loudness * one(*cut)
    return loudness


def scatter_about(stream_key, extent, width, limit, pieces=(), kind=jnp.bfloat16):
    result = width * jax.random.normal(stream_key, extent, jnp.float32)
    if pieces:
        result = result * level_of(stream_key, extent, pieces, -0.22, 0.18)
    return jnp.clip(result, -limit, limit).astype(kind)


def noise_with(key, dims, scale, most, cuts, heavy, held_as=jnp.bfloat16):
    entries = scale * jax.random.normal(key, dims, jnp.float32)
    if cuts:
        entries = entries * level_of(key, dims, cuts, -0.22, 0.18)
    return jnp.clip(with_spikes(entries, jax.random.fold_in(key, 3), *heavy), -most, most).astype(held_as)


def setup_inputs(seed: int = 0) -> dict:
    splits = jax.random.split(jax.random.key(seed), 4)
    grad_parts = noise_with(splits[0], (N_DP, LAYERS, KV_RANK, COLS), 1.0, 6.0, ((0, 2), (2, 4), (3, 4)), (0, 1, 2, 2.0))
    weight = scatter_about(splits[1], (LAYERS, KV_RANK, COLS), KV_RANK ** -0.5, 0.25, ((0, 2), (1, 4), (2, 4)))
    logit_max = jnp.clip(jnp.exp(math.log(1000.0) - 4.6051702 * jax.random.uniform(splits[2], (N_DP, N_CTX, LAYERS, HEADS), jnp.float32) ** level_of(splits[2], (N_DP, N_CTX, LAYERS, HEADS), ((0, 2), (1, 4)), -0.2, 0.2)), 10.0, 1000.0)
    return dict(grad_parts=grad_parts, weight=weight, logit_max=logit_max)


ns_a = 3.4445
ns_b = -4.775
ns_c = 2.0315
eps_norm = 1e-07
tau_clip = 100.0
learn_rate = 0.02
decay_rate = 0.1

def matmul(left, right):
    return jnp.dot(left, right, preferred_element_type=jnp.float32, precision=lax.Precision.HIGHEST)

def orthogonal(gradient):
    norm = jnp.sqrt(jnp.sum(gradient * gradient))
    x = gradient / (norm + eps_norm)
    for step in range(ITERS):
        gram = matmul(x, x.T)
        poly = ns_b * gram + ns_c * matmul(gram, gram)
        x = ns_a * x + matmul(poly, x)
    return x

def columns_of(head_factor):
    count = head_factor.shape[0]
    keys = jnp.broadcast_to(head_factor[:, None], (count, NOPE))
    values = jnp.ones((count, V_DIM), dtype=head_factor.dtype)
    return jnp.concatenate([keys, values], axis=1).reshape(-1)

def reference(grad_parts, weight, logit_max):
    scale = 0.2 * math.sqrt(max(KV_RANK, HEADS * (NOPE + V_DIM)))
    peak = lax.optimization_barrier(jnp.max(logit_max, axis=(0, 1)))
    factor = jnp.sqrt(jnp.minimum(1.0, tau_clip / peak))
    updates = []
    weights = []
    for layer in range(LAYERS):
        gradient = lax.optimization_barrier(jnp.sum(grad_parts[:, layer].astype(jnp.float32), axis=0))
        step_value = scale * orthogonal(gradient)
        column_factor = columns_of(factor[layer])
        fresh = (weight[layer].astype(jnp.float32) * (1.0 - learn_rate * decay_rate) - learn_rate * step_value) * column_factor[None, :]
        updates.append(step_value)
        weights.append(fresh)
    return (jnp.stack(updates), jnp.stack(weights))
```

```python
import functools
import math

import jax
import jax.numpy as jnp
from jax import lax
from jax.experimental import pallas as pl
from jax.experimental.pallas import tpu as pltpu
from jax.sharding import PartitionSpec as P

KV_RANK = 512
HEADS = 64
NOPE = 128
V_DIM = 128
ITERS = 2


ns_a = 3.4445
ns_b = -4.775
ns_c = 2.0315
eps_norm = 1e-07
tau_clip = 100.0
learn_rate = 0.02
decay_rate = 0.1

HEAD_COLS = NOPE + V_DIM
BLOCK = 128
SIDE = KV_RANK // BLOCK
PAIRS = [(i, j) for i in range(SIDE) for j in range(i, SIDE)]
UPDATE_SCALE = 0.2 * math.sqrt(max(KV_RANK, HEADS * HEAD_COLS))


def matmul(left, right):
    return jnp.dot(left, right, preferred_element_type=jnp.float32, precision=lax.Precision.HIGHEST)


def gram_sum(block):
    local = matmul(block, block.T)
    half = local.shape[0] // 2
    upper, corner = lax.psum((local[:half], local[half:, half:]), ("ctx", "fsdp"))
    lower = jnp.concatenate([upper[:, half:].T, corner], axis=1)
    return jnp.concatenate([upper, lower], axis=0)


def columns_of(head_factor):
    count = head_factor.shape[0]
    keys = jnp.broadcast_to(head_factor[:, None], (count, NOPE))
    values = jnp.ones((count, V_DIM), dtype=head_factor.dtype)
    return jnp.concatenate([keys, values], axis=1).reshape(-1)


def shards(grad_parts, weight, logit_max):
    parts = grad_parts[0].astype(jnp.float32)
    summed = lax.psum_scatter(parts, "dp", scatter_dimension=0, tiled=True)
    owned = lax.all_to_all(summed[0], "fsdp", split_axis=1, concat_axis=0, tiled=True)
    peak = lax.pmax(logit_max, ("dp", "ctx"))
    gram_raw = gram_sum(owned)
    denom = jnp.sqrt(jnp.trace(gram_raw)) + eps_norm
    iterate = owned / denom
    gram = gram_raw / (denom * denom)
    for step in range(ITERS):
        if step > 0:
            gram = gram_sum(iterate)
        poly = ns_b * gram + ns_c * matmul(gram, gram)
        iterate = ns_a * iterate + matmul(poly, iterate)
    step_value = UPDATE_SCALE * iterate
    back = lax.all_to_all(step_value, "fsdp", split_axis=0, concat_axis=1, tiled=True)
    layer_peak = lax.dynamic_index_in_dim(peak[0, 0], lax.axis_index("dp"), 0, keepdims=False)
    heads_here = HEADS // lax.axis_size("ctx")
    local_peak = lax.dynamic_slice_in_dim(
        layer_peak, lax.axis_index("ctx") * heads_here, heads_here, 0
    )
    factor = jnp.sqrt(jnp.minimum(1.0, tau_clip / local_peak))
    column_factor = columns_of(factor)
    fresh = (
        weight[0].astype(jnp.float32) * (1.0 - learn_rate * decay_rate) - learn_rate * back
    ) * column_factor[None, :]
    return (back[None], fresh[None])


def split(value):
    high = value.astype(jnp.bfloat16)
    low = (value - high.astype(jnp.float32)).astype(jnp.bfloat16)
    return high, low


def dot(left, right):
    return jnp.dot(left, right, preferred_element_type=jnp.float32)


def dot_nt(left, right):
    return lax.dot_general(
        left, right, (((1,), (1,)), ((), ())), preferred_element_type=jnp.float32
    )


def product(left, right):
    (lh, ll), (rh, rl) = left, right
    return dot(lh, rh) + (dot(lh, rl) + dot(ll, rh))


def gather_kernel(
    n_ctx, chunks,
    grad, logit, x_high, x_low, t_high, t_low, factor,
    outgoing, arriving, x_all, high_all, low_all, main, cross,
    packed, partial, total, gram, own_peak, peaks,
    y_send, y_recv, x_send, x_recv, c_send, c_recv, r_send, r_recv, out_sem,
    rs_send, rs_recv, ag_send, ag_recv, gx_send, gx_recv, gc_send, gc_recv, gr_send, gr_recv,
    pk_send, pk_recv,
):
    dp = lax.axis_index("dp")
    ctx = lax.axis_index("ctx")
    row = lax.axis_index("fsdp")
    other_dp = 1 - dp
    across = lax.rem(row + 2, 4)
    beside = row + 1 - 2 * lax.rem(row, 2)
    diagonal = lax.rem(beside + 2, 4)
    rows = grad.shape[1]

    def device(d, c, f):
        return {"dp": d, "ctx": c, "fsdp": f}

    def send(src, dst, send_sem, recv_sem, where):
        return pltpu.make_async_remote_copy(
            src_ref=src, dst_ref=dst, send_sem=send_sem, recv_sem=recv_sem,
            device_id=where, device_id_type=pl.DeviceIdType.MESH,
        )

    same = [
        (e, d) for e in range(2) for d in range(n_ctx) if (e, d) != (0, 0)
    ]

    def shifted(e, d):
        return device(lax.rem(dp + e, 2), lax.rem(ctx + d, n_ctx), row)

    barrier = pltpu.get_barrier_semaphore()
    for e, d in same:
        pl.semaphore_signal(barrier, 1, device_id=shifted(e, d), device_id_type=pl.DeviceIdType.MESH)
    for f in (across, beside):
        pl.semaphore_signal(barrier, 1, device_id=device(dp, ctx, f), device_id_type=pl.DeviceIdType.MESH)
    own_peak[...] = jnp.full(own_peak.shape, 10.0, jnp.float32)
    own_peak[0 : logit.shape[0], 0 : logit.shape[1]] = logit[...]
    pl.semaphore_wait(barrier, len(same) + 2)

    def block_of(f):
        return pl.ds(pl.multiple_of(f * rows, rows), rows)

    def y_copy(k):
        return send(
            outgoing.at[k], arriving.at[k], y_send.at[k], y_recv.at[k], device(other_dp, ctx, row)
        )

    def x_copy(k, f):
        part = x_all.at[k, block_of(f)]
        return send(part, part, x_send.at[k], x_recv.at[k], device(dp, ctx, across))

    def c_copy(k, f):
        part = x_all.at[k, block_of(f)]
        return send(part, part, c_send.at[k], c_recv.at[k], device(dp, ctx, beside))

    def r_copy(k, f):
        part = x_all.at[k, block_of(f)]
        return send(part, part, r_send.at[k], r_recv.at[k], device(dp, ctx, beside))

    def columns(k):
        return pl.ds(pl.multiple_of(k * HEAD_COLS, HEAD_COLS), HEAD_COLS)

    def out_copies(k):
        return (
            pltpu.make_async_copy(high_all.at[k], x_high.at[k], out_sem.at[0, k]),
            pltpu.make_async_copy(low_all.at[k], x_low.at[k], out_sem.at[1, k]),
        )

    def first(k, carry):
        @pl.when(k < chunks)
        def _():
            outgoing[k] = grad[other_dp, :, columns(k)].astype(jnp.float32)

        @pl.when(k >= 1)
        def _():
            y_copy(k - 1).start()

        return carry

    lax.fori_loop(0, chunks + 1, first, 0)

    def peak_copy(slot, e, d):
        return send(own_peak, peaks.at[slot], pk_send.at[slot], pk_recv.at[slot], shifted(e, d))

    for slot, (e, d) in enumerate(same):
        peak_copy(slot, e, d).start()

    main[...] = jnp.zeros_like(main)
    cross[...] = jnp.zeros_like(cross)

    def step(s, carry):
        @pl.when(s < chunks)
        def _():
            y_copy(s).wait_recv()
            x_all[s, block_of(row)] = (
                grad[dp, :, columns(s)].astype(jnp.float32) + arriving[s]
            )
            x_copy(s, row).start()
            c_copy(s, row).start()

        @pl.when((s >= 2) & (s < chunks + 2))
        def _():
            k = s - 2
            x_copy(k, across).wait_recv()
            r_copy(k, across).start()

        @pl.when(s >= 3)
        def _():
            k = s - 3
            c_copy(k, beside).wait_recv()
            r_copy(k, diagonal).wait_recv()
            high, low = split(x_all[k])
            high_all[k] = high
            low_all[k] = low
            main[...] += dot_nt(high, high)
            cross[...] += dot_nt(high, low)
            for copy in out_copies(k):
                copy.start()

        return carry

    lax.fori_loop(0, chunks + 3, step, 0)

    def tile(ref, i, j):
        return ref[i * BLOCK : (i + 1) * BLOCK, j * BLOCK : (j + 1) * BLOCK]

    for b, (i, j) in enumerate(PAIRS):
        packed[b * BLOCK : (b + 1) * BLOCK] = (
            tile(main, i, j) + tile(cross, i, j) + tile(cross, j, i).T
        )

    piece = len(PAIRS) * BLOCK // (4 * n_ctx)

    def piece_of(f, c):
        return pl.ds(pl.multiple_of((f * n_ctx + c) * piece, 8), piece)

    def ahead(d):
        return lax.rem(ctx + d, n_ctx)

    def behind(d):
        return lax.rem(ctx + n_ctx - d, n_ctx)

    def rs_copy(d):
        return send(
            packed.at[piece_of(row, ahead(d))], partial.at[d],
            rs_send.at[d], rs_recv.at[d], device(dp, ahead(d), row),
        )

    for d in range(1, n_ctx):
        rs_copy(d).start()
    mine = packed[piece_of(row, ctx)]
    for d in range(1, n_ctx):
        rs_copy(d).wait_recv()
        mine = mine + partial[d]
    total[piece_of(row, ctx)] = mine

    def ag_copy(d, c):
        part = total.at[piece_of(row, c)]
        return send(part, part, ag_send.at[d], ag_recv.at[d], device(dp, ahead(d), row))

    def gx_copy(d, f):
        part = total.at[piece_of(f, behind(d))]
        return send(part, part, gx_send.at[d], gx_recv.at[d], device(dp, ctx, across))

    def gc_copy(d, f):
        part = total.at[piece_of(f, behind(d))]
        return send(part, part, gc_send.at[d], gc_recv.at[d], device(dp, ctx, beside))

    def gr_copy(d, f):
        part = total.at[piece_of(f, behind(d))]
        return send(part, part, gr_send.at[d], gr_recv.at[d], device(dp, ctx, beside))

    for d in range(1, n_ctx):
        ag_copy(d, ctx).start()
    for d in range(n_ctx):
        if d > 0:
            ag_copy(d, behind(d)).wait_recv()
        gx_copy(d, row).start()
        gc_copy(d, row).start()
    for d in range(n_ctx):
        gx_copy(d, across).wait_recv()
        gr_copy(d, across).start()

    top = own_peak[...]
    for slot, (e, d) in enumerate(same):
        peak_copy(slot, e, d).wait_recv()
        top = jnp.maximum(top, peaks[slot])
    factor[...] = jnp.sqrt(jnp.minimum(1.0, tau_clip / top))

    for d in range(n_ctx):
        gc_copy(d, beside).wait_recv()
        gr_copy(d, diagonal).wait_recv()

    near = lax.broadcasted_iota(jnp.int32, (BLOCK, BLOCK), 0) == lax.broadcasted_iota(
        jnp.int32, (BLOCK, BLOCK), 1
    )
    diag = jnp.zeros((BLOCK, BLOCK), jnp.float32)
    for b, (i, j) in enumerate(PAIRS):
        if i == j:
            diag = diag + jnp.where(near, total[b * BLOCK : (b + 1) * BLOCK], 0.0)
    trace = jnp.sum(jnp.sum(diag, axis=0, keepdims=True), axis=1, keepdims=True)
    denom = jnp.sqrt(trace) + eps_norm
    squared = denom * denom
    for b, (i, j) in enumerate(PAIRS):
        value = total[b * BLOCK : (b + 1) * BLOCK] / squared
        gram[i * BLOCK : (i + 1) * BLOCK, j * BLOCK : (j + 1) * BLOCK] = value
        if i != j:
            gram[j * BLOCK : (j + 1) * BLOCK, i * BLOCK : (i + 1) * BLOCK] = value.T

    eye = lax.broadcasted_iota(jnp.int32, gram.shape, 0) == lax.broadcasted_iota(
        jnp.int32, gram.shape, 1
    )
    g = gram[...]
    g_parts = split(g)
    poly = ns_b * g + ns_c * product(g_parts, g_parts)
    q0_parts = split(poly + jnp.where(eye, ns_a, 0.0))
    later = product(split(product(g_parts, q0_parts)), q0_parts)
    gram[...] = later
    some = gram[block_of(row)]
    spot = lax.broadcasted_iota(jnp.int32, some.shape, 0) + row * rows == lax.broadcasted_iota(
        jnp.int32, some.shape, 1
    )
    poly = ns_b * some + ns_c * product(split(some), split(later))
    q1 = poly + jnp.where(spot, ns_a, 0.0)
    t = product(split(q1), q0_parts) * (UPDATE_SCALE / denom)
    high, low = split(t)
    t_high[...] = high
    t_low[...] = low

    def last(k, carry):
        y_copy(k).wait_send()
        x_copy(k, row).wait_send()
        c_copy(k, row).wait_send()
        r_copy(k, across).wait_send()
        for copy in out_copies(k):
            copy.wait()
        return carry

    lax.fori_loop(0, chunks, last, 0)
    for slot, (e, d) in enumerate(same):
        peak_copy(slot, e, d).wait_send()
    for d in range(n_ctx):
        if d > 0:
            rs_copy(d).wait_send()
            ag_copy(d, ctx).wait_send()
        gx_copy(d, row).wait_send()
        gc_copy(d, row).wait_send()
        gr_copy(d, across).wait_send()


def gather(grad, logit, n_ctx):
    _, rows, cols = grad.shape
    chunks = cols // HEAD_COLS
    f32, bf16 = jnp.float32, jnp.bfloat16
    sem = pltpu.SemaphoreType.DMA
    packed_rows = len(PAIRS) * BLOCK
    vmem = pl.BlockSpec(memory_space=pltpu.VMEM)
    anywhere = pl.BlockSpec(memory_space=pl.ANY)
    wide = (chunks, KV_RANK, HEAD_COLS)
    return pl.pallas_call(
        functools.partial(gather_kernel, n_ctx, chunks),
        out_shape=(
            jax.ShapeDtypeStruct(wide, bf16),
            jax.ShapeDtypeStruct(wide, bf16),
            jax.ShapeDtypeStruct((rows, KV_RANK), bf16),
            jax.ShapeDtypeStruct((rows, KV_RANK), bf16),
            jax.ShapeDtypeStruct((8, 128), f32),
        ),
        in_specs=[vmem, vmem],
        out_specs=(anywhere, anywhere, vmem, vmem, vmem),
        scratch_shapes=[
            pltpu.VMEM((chunks, rows, HEAD_COLS), f32),
            pltpu.VMEM((chunks, rows, HEAD_COLS), f32),
            pltpu.VMEM(wide, f32),
            pltpu.VMEM(wide, bf16),
            pltpu.VMEM(wide, bf16),
            pltpu.VMEM((KV_RANK, KV_RANK), f32),
            pltpu.VMEM((KV_RANK, KV_RANK), f32),
            pltpu.VMEM((packed_rows, BLOCK), f32),
            pltpu.VMEM((n_ctx, packed_rows // (4 * n_ctx), BLOCK), f32),
            pltpu.VMEM((packed_rows, BLOCK), f32),
            pltpu.VMEM((KV_RANK, KV_RANK), f32),
            pltpu.VMEM((8, 128), f32),
            pltpu.VMEM((2 * n_ctx - 1, 8, 128), f32),
        ]
        + [sem((chunks,))] * 8
        + [sem((2, chunks))]
        + [sem((n_ctx,))] * 10
        + [sem((2 * n_ctx - 1,))] * 2,
        compiler_params=pltpu.CompilerParams(
            collective_id=0, has_side_effects=True, vmem_limit_bytes=56 * 1024 * 1024
        ),
    )(grad, logit)


def apply_kernel(heads, factor, t_high, t_low, x_high, x_low, weight, update, fresh):
    layer = lax.axis_index("dp")
    base = lax.axis_index("ctx") * (heads * pl.num_programs(0)) + pl.program_id(0) * heads
    keep = 1.0 - learn_rate * decay_rate
    for h in range(heads):
        value = product((t_high[...], t_low[...]), (x_high[h], x_low[h]))
        start = h * HEAD_COLS
        update[0, :, start : start + HEAD_COLS] = value
        old = weight[0, :, start : start + HEAD_COLS].astype(jnp.float32)
        moved = old * keep - learn_rate * value
        fresh[0, :, start : start + NOPE] = moved[:, :NOPE] * factor[layer, base + h]
        fresh[0, :, start + NOPE : start + HEAD_COLS] = moved[:, NOPE:]


def apply(factor, t_high, t_low, x_high, x_low, weight, heads):
    chunks = x_high.shape[0]
    rows = weight.shape[1]
    shape = jax.ShapeDtypeStruct(weight.shape, jnp.float32)
    whole = pl.BlockSpec((rows, KV_RANK), lambda i: (0, 0))
    stream = pl.BlockSpec((heads, KV_RANK, HEAD_COLS), lambda i: (i, 0, 0))
    flat = pl.BlockSpec((1, rows, heads * HEAD_COLS), lambda i: (0, 0, i))
    return pl.pallas_call(
        functools.partial(apply_kernel, heads),
        grid=(chunks // heads,),
        out_shape=(shape, shape),
        in_specs=[pl.BlockSpec(memory_space=pltpu.SMEM), whole, whole, stream, stream, flat],
        out_specs=(flat, flat),
    )(factor, t_high, t_low, x_high, x_low, weight)


def kernel_shards(n_ctx, grad_parts, weight, logit_max):
    x_high, x_low, t_high, t_low, factor = gather(grad_parts[0], logit_max[0, 0], n_ctx)
    return apply(factor, t_high, t_low, x_high, x_low, weight, 2)


def solution(mesh):
    fits = mesh.shape["dp"] == 2 and mesh.shape["fsdp"] == 4 and mesh.shape["ctx"] <= 8
    body = functools.partial(kernel_shards, mesh.shape["ctx"]) if fits else shards
    return jax.shard_map(
        body,
        mesh=mesh,
        in_specs=(P("dp", None, "fsdp", "ctx"), P("dp", "fsdp", "ctx"), P("dp", "ctx", None, None)),
        out_specs=(P("dp", "fsdp", "ctx"), P("dp", "fsdp", "ctx")),
        check_vma=False,
    )
```

```python
import functools
import math

import jax
import jax.numpy as jnp
from jax import lax
from jax.experimental import pallas as pl
from jax.experimental.pallas import tpu as pltpu
from jax.sharding import PartitionSpec as P

KV_RANK = 512
HEADS = 64
NOPE = 128
V_DIM = 128
ITERS = 2


ns_a = 3.4445
ns_b = -4.775
ns_c = 2.0315
eps_norm = 1e-07
tau_clip = 100.0
learn_rate = 0.02
decay_rate = 0.1

HEAD_COLS = NOPE + V_DIM
BLOCK = 128
CHUNK = 128
CUTS = 2
JOIN = HEAD_COLS // CHUNK
SIDE = KV_RANK // BLOCK
PAIRS = [(i, j) for i in range(SIDE) for j in range(i, SIDE)]
UPDATE_SCALE = 0.2 * math.sqrt(max(KV_RANK, HEADS * HEAD_COLS))


def matmul(left, right):
    return jnp.dot(left, right, preferred_element_type=jnp.float32, precision=lax.Precision.HIGHEST)


def gram_sum(block):
    local = matmul(block, block.T)
    half = local.shape[0] // 2
    upper, corner = lax.psum((local[:half], local[half:, half:]), ("ctx", "fsdp"))
    lower = jnp.concatenate([upper[:, half:].T, corner], axis=1)
    return jnp.concatenate([upper, lower], axis=0)


def columns_of(head_factor):
    count = head_factor.shape[0]
    keys = jnp.broadcast_to(head_factor[:, None], (count, NOPE))
    values = jnp.ones((count, V_DIM), dtype=head_factor.dtype)
    return jnp.concatenate([keys, values], axis=1).reshape(-1)


def shards(grad_parts, weight, logit_max):
    parts = grad_parts[0].astype(jnp.float32)
    summed = lax.psum_scatter(parts, "dp", scatter_dimension=0, tiled=True)
    owned = lax.all_to_all(summed[0], "fsdp", split_axis=1, concat_axis=0, tiled=True)
    peak = lax.pmax(logit_max, ("dp", "ctx"))
    gram_raw = gram_sum(owned)
    denom = jnp.sqrt(jnp.trace(gram_raw)) + eps_norm
    iterate = owned / denom
    gram = gram_raw / (denom * denom)
    for step in range(ITERS):
        if step > 0:
            gram = gram_sum(iterate)
        poly = ns_b * gram + ns_c * matmul(gram, gram)
        iterate = ns_a * iterate + matmul(poly, iterate)
    step_value = UPDATE_SCALE * iterate
    back = lax.all_to_all(step_value, "fsdp", split_axis=0, concat_axis=1, tiled=True)
    layer_peak = lax.dynamic_index_in_dim(peak[0, 0], lax.axis_index("dp"), 0, keepdims=False)
    heads_here = HEADS // lax.axis_size("ctx")
    local_peak = lax.dynamic_slice_in_dim(
        layer_peak, lax.axis_index("ctx") * heads_here, heads_here, 0
    )
    factor = jnp.sqrt(jnp.minimum(1.0, tau_clip / local_peak))
    column_factor = columns_of(factor)
    fresh = (
        weight[0].astype(jnp.float32) * (1.0 - learn_rate * decay_rate) - learn_rate * back
    ) * column_factor[None, :]
    return (back[None], fresh[None])


def split(value):
    high = value.astype(jnp.bfloat16)
    low = (value - high.astype(jnp.float32)).astype(jnp.bfloat16)
    return high, low


def dot(left, right):
    return jnp.dot(left, right, preferred_element_type=jnp.float32)


def dot_nt(left, right):
    return lax.dot_general(
        left, right, (((1,), (1,)), ((), ())), preferred_element_type=jnp.float32
    )


def product(left, right):
    (lh, ll), (rh, rl) = left, right
    return dot(lh, rh) + (dot(lh, rl) + dot(ll, rh))


def gather_kernel(
    n_ctx, chunks, cuts,
    grad, logit, x_high, x_low, t_high, t_low, factor,
    grads, outgoing, arriving, x_all, high_all, low_all, main, cross,
    packed, partial, total, gram, own_peak, peaks,
    y_send, y_recv, x_send, x_recv, c_send, c_recv, r_send, r_recv, out_sem,
    rs_send, rs_recv, ag_send, ag_recv, gx_send, gx_recv, gc_send, gc_recv, gr_send, gr_recv,
    pk_send, pk_recv, in_sem,
):
    dp = lax.axis_index("dp")
    ctx = lax.axis_index("ctx")
    row = lax.axis_index("fsdp")
    other_dp = 1 - dp
    across = lax.rem(row + 2, 4)
    beside = row + 1 - 2 * lax.rem(row, 2)
    diagonal = lax.rem(beside + 2, 4)
    rows = grad.shape[1]
    loads = [
        pltpu.make_async_copy(grad.at[layer], grads.at[layer], in_sem.at[i])
        for i, layer in enumerate((other_dp, dp))
    ]
    for load in loads:
        load.start()

    def device(d, c, f):
        return {"dp": d, "ctx": c, "fsdp": f}

    def send(src, dst, send_sem, recv_sem, where):
        return pltpu.make_async_remote_copy(
            src_ref=src, dst_ref=dst, send_sem=send_sem, recv_sem=recv_sem,
            device_id=where, device_id_type=pl.DeviceIdType.MESH,
        )

    same = [
        (e, d) for e in range(2) for d in range(n_ctx) if (e, d) != (0, 0)
    ]

    def shifted(e, d):
        return device(lax.rem(dp + e, 2), lax.rem(ctx + d, n_ctx), row)

    barrier = pltpu.get_barrier_semaphore()
    for e, d in same:
        pl.semaphore_signal(barrier, 1, device_id=shifted(e, d), device_id_type=pl.DeviceIdType.MESH)
    for f in (across, beside):
        pl.semaphore_signal(barrier, 1, device_id=device(dp, ctx, f), device_id_type=pl.DeviceIdType.MESH)
    own_peak[...] = jnp.full(own_peak.shape, 10.0, jnp.float32)
    own_peak[0 : logit.shape[0], 0 : logit.shape[1]] = logit[...]
    pl.semaphore_wait(barrier, len(same) + 2)

    def block_of(f):
        return pl.ds(pl.multiple_of(f * rows, rows), rows)

    def y_copy(k):
        return send(
            outgoing.at[k], arriving.at[k], y_send.at[k], y_recv.at[k], device(other_dp, ctx, row)
        )

    def x_copy(k, f):
        part = x_all.at[k, block_of(f)]
        return send(part, part, x_send.at[k], x_recv.at[k], device(dp, ctx, across))

    def c_copy(k, f):
        part = x_all.at[k, block_of(f)]
        return send(part, part, c_send.at[k], c_recv.at[k], device(dp, ctx, beside))

    def r_copy(k, f):
        part = x_all.at[k, block_of(f)]
        return send(part, part, r_send.at[k], r_recv.at[k], device(dp, ctx, beside))

    def columns(k):
        return pl.ds(pl.multiple_of(k * CHUNK, CHUNK), CHUNK)

    def out_copies(k):
        return (
            pltpu.make_async_copy(high_all.at[k], x_high.at[k], out_sem.at[0, k]),
            pltpu.make_async_copy(low_all.at[k], x_low.at[k], out_sem.at[1, k]),
        )

    def first(k, carry):
        @pl.when(k < chunks)
        def _():
            outgoing[k] = grads[other_dp, :, columns(k)].astype(jnp.float32)

        @pl.when(k >= 1)
        def _():
            y_copy(k - 1).start()

        return carry

    loads[0].wait()
    lax.fori_loop(0, chunks + 1, first, 0)

    def peak_copy(slot, e, d):
        return send(own_peak, peaks.at[slot], pk_send.at[slot], pk_recv.at[slot], shifted(e, d))

    for slot, (e, d) in enumerate(same):
        peak_copy(slot, e, d).start()

    main[...] = jnp.zeros_like(main)
    cross[...] = jnp.zeros_like(cross)

    loads[1].wait()

    def step(s, carry):
        @pl.when(s < chunks)
        def _():
            y_copy(s).wait_recv()
            x_all[s, block_of(row)] = (
                grads[dp, :, columns(s)].astype(jnp.float32) + arriving[s]
            )
            x_copy(s, row).start()
            c_copy(s, row).start()

        @pl.when((s >= 2) & (s < chunks + 2))
        def _():
            k = s - 2
            x_copy(k, across).wait_recv()
            r_copy(k, across).start()

        @pl.when(s >= 3)
        def _():
            k = s - 3
            c_copy(k, beside).wait_recv()
            r_copy(k, diagonal).wait_recv()

            @pl.when(lax.rem(k, JOIN) == JOIN - 1)
            def _():
                head = lax.div(k, JOIN)
                value = jnp.concatenate(
                    [x_all[head * JOIN + i] for i in range(JOIN)], axis=1
                )
                high, low = split(value)
                high_all[head] = high
                low_all[head] = low
                main[...] += dot_nt(high, high)
                cross[...] += dot_nt(high, low)
                for copy in out_copies(head):
                    copy.start()

        return carry

    lax.fori_loop(0, chunks + 3, step, 0)

    def tile(ref, i, j):
        return ref[i * BLOCK : (i + 1) * BLOCK, j * BLOCK : (j + 1) * BLOCK]

    quarter = len(PAIRS) * BLOCK // 4
    for f in range(4):

        @pl.when(row == f)
        def _(f=f):
            for b, (i, j) in enumerate(PAIRS):
                if b * BLOCK < (f + 1) * quarter and (b + 1) * BLOCK > f * quarter:
                    packed[b * BLOCK : (b + 1) * BLOCK] = (
                        tile(main, i, j) + tile(cross, i, j) + tile(cross, j, i).T
                    )

    piece = quarter // n_ctx
    part_rows = piece // cuts

    def piece_of(f, c, h):
        start = (f * n_ctx + c) * piece + h * part_rows
        return pl.ds(pl.multiple_of(start, 8), part_rows)

    def ahead(d):
        return lax.rem(ctx + d, n_ctx)

    def behind(d):
        return lax.rem(ctx + n_ctx - d, n_ctx)

    def rs_copy(h, d):
        n = h * n_ctx + d
        return send(
            packed.at[piece_of(row, ahead(d), h)], partial.at[n],
            rs_send.at[n], rs_recv.at[n], device(dp, ahead(d), row),
        )

    def ag_copy(h, d, c):
        n = h * n_ctx + d
        part = total.at[piece_of(row, c, h)]
        return send(part, part, ag_send.at[n], ag_recv.at[n], device(dp, ahead(d), row))

    def gx_copy(h, d, f):
        n = h * n_ctx + d
        part = total.at[piece_of(f, behind(d), h)]
        return send(part, part, gx_send.at[n], gx_recv.at[n], device(dp, ctx, across))

    def gc_copy(h, d, f):
        n = h * n_ctx + d
        part = total.at[piece_of(f, behind(d), h)]
        return send(part, part, gc_send.at[n], gc_recv.at[n], device(dp, ctx, beside))

    def gr_copy(h, d, f):
        n = h * n_ctx + d
        part = total.at[piece_of(f, behind(d), h)]
        return send(part, part, gr_send.at[n], gr_recv.at[n], device(dp, ctx, beside))

    for h in range(cuts):
        for d in range(1, n_ctx):
            rs_copy(h, d).start()
    for h in range(cuts):
        mine = packed[piece_of(row, ctx, h)]
        for d in range(1, n_ctx):
            rs_copy(h, d).wait_recv()
            mine = mine + partial[h * n_ctx + d]
        total[piece_of(row, ctx, h)] = mine
        for d in range(1, n_ctx):
            ag_copy(h, d, ctx).start()
        gx_copy(h, 0, row).start()
        gc_copy(h, 0, row).start()
    for h in range(cuts):
        for d in range(1, n_ctx):
            ag_copy(h, d, behind(d)).wait_recv()
            gx_copy(h, d, row).start()
            gc_copy(h, d, row).start()
    for h in range(cuts):
        for d in range(n_ctx):
            gx_copy(h, d, across).wait_recv()
            gr_copy(h, d, across).start()

    top = own_peak[...]
    for slot, (e, d) in enumerate(same):
        peak_copy(slot, e, d).wait_recv()
        top = jnp.maximum(top, peaks[slot])
    factor[...] = jnp.sqrt(jnp.minimum(1.0, tau_clip / top))

    for h in range(cuts):
        for d in range(n_ctx):
            gc_copy(h, d, beside).wait_recv()
            gr_copy(h, d, diagonal).wait_recv()

    near = lax.broadcasted_iota(jnp.int32, (BLOCK, BLOCK), 0) == lax.broadcasted_iota(
        jnp.int32, (BLOCK, BLOCK), 1
    )
    diag = jnp.zeros((BLOCK, BLOCK), jnp.float32)
    for b, (i, j) in enumerate(PAIRS):
        if i == j:
            diag = diag + jnp.where(near, total[b * BLOCK : (b + 1) * BLOCK], 0.0)
    trace = jnp.sum(jnp.sum(diag, axis=0, keepdims=True), axis=1, keepdims=True)
    denom = jnp.sqrt(trace) + eps_norm
    squared = denom * denom
    for b, (i, j) in enumerate(PAIRS):
        value = total[b * BLOCK : (b + 1) * BLOCK] / squared
        gram[i * BLOCK : (i + 1) * BLOCK, j * BLOCK : (j + 1) * BLOCK] = value
        if i != j:
            gram[j * BLOCK : (j + 1) * BLOCK, i * BLOCK : (i + 1) * BLOCK] = value.T

    eye = lax.broadcasted_iota(jnp.int32, gram.shape, 0) == lax.broadcasted_iota(
        jnp.int32, gram.shape, 1
    )
    g = gram[...]
    g_parts = split(g)
    poly = ns_b * g + ns_c * product(g_parts, g_parts)
    q0_parts = split(poly + jnp.where(eye, ns_a, 0.0))
    later = product(split(product(g_parts, q0_parts)), q0_parts)
    gram[...] = later
    some = gram[block_of(row)]
    spot = lax.broadcasted_iota(jnp.int32, some.shape, 0) + row * rows == lax.broadcasted_iota(
        jnp.int32, some.shape, 1
    )
    poly = ns_b * some + ns_c * product(split(some), split(later))
    q1 = poly + jnp.where(spot, ns_a, 0.0)
    t = product(split(q1), q0_parts) * (UPDATE_SCALE / denom)
    high, low = split(t)
    t_high[...] = high
    t_low[...] = low

    def last(k, carry):
        y_copy(k).wait_send()
        x_copy(k, row).wait_send()
        c_copy(k, row).wait_send()
        r_copy(k, across).wait_send()
        return carry

    lax.fori_loop(0, chunks, last, 0)
    for head in range(chunks // JOIN):
        for copy in out_copies(head):
            copy.wait()
    for slot, (e, d) in enumerate(same):
        peak_copy(slot, e, d).wait_send()
    for h in range(cuts):
        for d in range(n_ctx):
            if d > 0:
                rs_copy(h, d).wait_send()
                ag_copy(h, d, ctx).wait_send()
            gx_copy(h, d, row).wait_send()
            gc_copy(h, d, row).wait_send()
            gr_copy(h, d, across).wait_send()


def cuts_of(n_ctx):
    piece = len(PAIRS) * BLOCK // (4 * n_ctx)
    return CUTS if piece % (8 * CUTS) == 0 else 1


def gather(grad, logit, n_ctx):
    _, rows, cols = grad.shape
    chunks = cols // CHUNK
    heads = cols // HEAD_COLS
    cuts = cuts_of(n_ctx)
    f32, bf16 = jnp.float32, jnp.bfloat16
    sem = pltpu.SemaphoreType.DMA
    packed_rows = len(PAIRS) * BLOCK
    vmem = pl.BlockSpec(memory_space=pltpu.VMEM)
    anywhere = pl.BlockSpec(memory_space=pl.ANY)
    wide = (heads, KV_RANK, HEAD_COLS)
    return pl.pallas_call(
        functools.partial(gather_kernel, n_ctx, chunks, cuts),
        out_shape=(
            jax.ShapeDtypeStruct(wide, bf16),
            jax.ShapeDtypeStruct(wide, bf16),
            jax.ShapeDtypeStruct((rows, KV_RANK), bf16),
            jax.ShapeDtypeStruct((rows, KV_RANK), bf16),
            jax.ShapeDtypeStruct((8, 128), f32),
        ),
        in_specs=[anywhere, vmem],
        out_specs=(anywhere, anywhere, vmem, vmem, vmem),
        scratch_shapes=[
            pltpu.VMEM(grad.shape, bf16),
            pltpu.VMEM((chunks, rows, CHUNK), f32),
            pltpu.VMEM((chunks, rows, CHUNK), f32),
            pltpu.VMEM((chunks, KV_RANK, CHUNK), f32),
            pltpu.VMEM(wide, bf16),
            pltpu.VMEM(wide, bf16),
            pltpu.VMEM((KV_RANK, KV_RANK), f32),
            pltpu.VMEM((KV_RANK, KV_RANK), f32),
            pltpu.VMEM((packed_rows, BLOCK), f32),
            pltpu.VMEM((cuts * n_ctx, packed_rows // (4 * n_ctx * cuts), BLOCK), f32),
            pltpu.VMEM((packed_rows, BLOCK), f32),
            pltpu.VMEM((KV_RANK, KV_RANK), f32),
            pltpu.VMEM((8, 128), f32),
            pltpu.VMEM((2 * n_ctx - 1, 8, 128), f32),
        ]
        + [sem((chunks,))] * 8
        + [sem((2, heads))]
        + [sem((cuts * n_ctx,))] * 10
        + [sem((2 * n_ctx - 1,))] * 2
        + [sem((2,))],
        compiler_params=pltpu.CompilerParams(
            collective_id=0, has_side_effects=True, vmem_limit_bytes=36 * 1024 * 1024
        ),
    )(grad, logit)


def apply_kernel(heads, factor, t_high, t_low, x_high, x_low, weight, update, fresh):
    layer = lax.axis_index("dp")
    base = lax.axis_index("ctx") * (heads * pl.num_programs(0)) + pl.program_id(0) * heads
    keep = 1.0 - learn_rate * decay_rate
    for h in range(heads):
        value = product((t_high[...], t_low[...]), (x_high[h], x_low[h]))
        start = h * HEAD_COLS
        update[0, :, start : start + HEAD_COLS] = value
        old = weight[0, :, start : start + HEAD_COLS].astype(jnp.float32)
        moved = old * keep - learn_rate * value
        fresh[0, :, start : start + NOPE] = moved[:, :NOPE] * factor[layer, base + h]
        fresh[0, :, start + NOPE : start + HEAD_COLS] = moved[:, NOPE:]


def apply(factor, t_high, t_low, x_high, x_low, weight, heads):
    chunks = x_high.shape[0]
    rows = weight.shape[1]
    shape = jax.ShapeDtypeStruct(weight.shape, jnp.float32)
    whole = pl.BlockSpec((rows, KV_RANK), lambda i: (0, 0))
    stream = pl.BlockSpec((heads, KV_RANK, HEAD_COLS), lambda i: (i, 0, 0))
    flat = pl.BlockSpec((1, rows, heads * HEAD_COLS), lambda i: (0, 0, i))
    return pl.pallas_call(
        functools.partial(apply_kernel, heads),
        grid=(chunks // heads,),
        out_shape=(shape, shape),
        in_specs=[pl.BlockSpec(memory_space=pltpu.SMEM), whole, whole, stream, stream, flat],
        out_specs=(flat, flat),
        compiler_params=pltpu.CompilerParams(vmem_limit_bytes=20 * 1024 * 1024),
    )(factor, t_high, t_low, x_high, x_low, weight)


def kernel_shards(n_ctx, grad_parts, weight, logit_max):
    x_high, x_low, t_high, t_low, factor = gather(grad_parts[0], logit_max[0, 0], n_ctx)
    return apply(factor, t_high, t_low, x_high, x_low, weight, 4)


def solution(mesh):
    fits = mesh.shape["dp"] == 2 and mesh.shape["fsdp"] == 4 and mesh.shape["ctx"] <= 8
    body = functools.partial(kernel_shards, mesh.shape["ctx"]) if fits else shards
    return jax.shard_map(
        body,
        mesh=mesh,
        in_specs=(P("dp", None, "fsdp", "ctx"), P("dp", "fsdp", "ctx"), P("dp", "ctx", None, None)),
        out_specs=(P("dp", "fsdp", "ctx"), P("dp", "fsdp", "ctx")),
        check_vma=False,
    )
```

```python
import functools
import math

import jax
import jax.numpy as jnp
from jax import lax
from jax.experimental import pallas as pl
from jax.experimental.pallas import tpu as pltpu
from jax.sharding import PartitionSpec as P

KV_RANK = 512
HEADS = 64
NOPE = 128
V_DIM = 128
ITERS = 2


ns_a = 3.4445
ns_b = -4.775
ns_c = 2.0315
eps_norm = 1e-07
tau_clip = 100.0
learn_rate = 0.02
decay_rate = 0.1

HEAD_COLS = NOPE + V_DIM
BLOCK = 128
CHUNK = 128
CUTS = 2
JOIN = HEAD_COLS // CHUNK
SIDE = KV_RANK // BLOCK
PAIRS = [(i, j) for i in range(SIDE) for j in range(i, SIDE)]
UPDATE_SCALE = 0.2 * math.sqrt(max(KV_RANK, HEADS * HEAD_COLS))


def matmul(left, right):
    return jnp.dot(left, right, preferred_element_type=jnp.float32, precision=lax.Precision.HIGHEST)


def gram_sum(block):
    local = matmul(block, block.T)
    half = local.shape[0] // 2
    upper, corner = lax.psum((local[:half], local[half:, half:]), ("ctx", "fsdp"))
    lower = jnp.concatenate([upper[:, half:].T, corner], axis=1)
    return jnp.concatenate([upper, lower], axis=0)


def columns_of(head_factor):
    count = head_factor.shape[0]
    keys = jnp.broadcast_to(head_factor[:, None], (count, NOPE))
    values = jnp.ones((count, V_DIM), dtype=head_factor.dtype)
    return jnp.concatenate([keys, values], axis=1).reshape(-1)


def shards(grad_parts, weight, logit_max):
    parts = grad_parts[0].astype(jnp.float32)
    summed = lax.psum_scatter(parts, "dp", scatter_dimension=0, tiled=True)
    owned = lax.all_to_all(summed[0], "fsdp", split_axis=1, concat_axis=0, tiled=True)
    peak = lax.pmax(logit_max, ("dp", "ctx"))
    gram_raw = gram_sum(owned)
    denom = jnp.sqrt(jnp.trace(gram_raw)) + eps_norm
    iterate = owned / denom
    gram = gram_raw / (denom * denom)
    for step in range(ITERS):
        if step > 0:
            gram = gram_sum(iterate)
        poly = ns_b * gram + ns_c * matmul(gram, gram)
        iterate = ns_a * iterate + matmul(poly, iterate)
    step_value = UPDATE_SCALE * iterate
    back = lax.all_to_all(step_value, "fsdp", split_axis=0, concat_axis=1, tiled=True)
    layer_peak = lax.dynamic_index_in_dim(peak[0, 0], lax.axis_index("dp"), 0, keepdims=False)
    heads_here = HEADS // lax.axis_size("ctx")
    local_peak = lax.dynamic_slice_in_dim(
        layer_peak, lax.axis_index("ctx") * heads_here, heads_here, 0
    )
    factor = jnp.sqrt(jnp.minimum(1.0, tau_clip / local_peak))
    column_factor = columns_of(factor)
    fresh = (
        weight[0].astype(jnp.float32) * (1.0 - learn_rate * decay_rate) - learn_rate * back
    ) * column_factor[None, :]
    return (back[None], fresh[None])


def split(value):
    high = value.astype(jnp.bfloat16)
    low = (value - high.astype(jnp.float32)).astype(jnp.bfloat16)
    return high, low


def dot(left, right):
    return jnp.dot(left, right, preferred_element_type=jnp.float32)


def dot_nt(left, right):
    return lax.dot_general(
        left, right, (((1,), (1,)), ((), ())), preferred_element_type=jnp.float32
    )


def product(left, right):
    (lh, ll), (rh, rl) = left, right
    return dot(lh, rh) + (dot(lh, rl) + dot(ll, rh))


def gather_kernel(
    n_ctx, chunks, cuts,
    grad, logit, x_high, x_low, t_high, t_low, factor,
    logits, grads, outgoing, arriving, x_all, high_all, low_all, main, cross,
    packed, partial, total, gram, own_peak, peaks,
    y_send, y_recv, x_send, x_recv, c_send, c_recv, r_send, r_recv, out_sem,
    rs_send, rs_recv, ag_send, ag_recv, gx_send, gx_recv, gc_send, gc_recv, gr_send, gr_recv,
    pk_send, pk_recv, in_sem,
):
    dp = lax.axis_index("dp")
    ctx = lax.axis_index("ctx")
    row = lax.axis_index("fsdp")
    other_dp = 1 - dp
    across = lax.rem(row + 2, 4)
    beside = row + 1 - 2 * lax.rem(row, 2)
    diagonal = lax.rem(beside + 2, 4)
    rows = grad.shape[1]
    loads = [
        pltpu.make_async_copy(grad.at[layer], grads.at[layer], in_sem.at[i])
        for i, layer in enumerate((other_dp, dp))
    ]
    loads.append(pltpu.make_async_copy(logit, logits, in_sem.at[2]))
    for load in loads:
        load.start()

    def device(d, c, f):
        return {"dp": d, "ctx": c, "fsdp": f}

    def send(src, dst, send_sem, recv_sem, where):
        return pltpu.make_async_remote_copy(
            src_ref=src, dst_ref=dst, send_sem=send_sem, recv_sem=recv_sem,
            device_id=where, device_id_type=pl.DeviceIdType.MESH,
        )

    same = [
        (e, d) for e in range(2) for d in range(n_ctx) if (e, d) != (0, 0)
    ]

    def shifted(e, d):
        return device(lax.rem(dp + e, 2), lax.rem(ctx + d, n_ctx), row)

    barrier = pltpu.get_barrier_semaphore()
    for e, d in same:
        pl.semaphore_signal(barrier, 1, device_id=shifted(e, d), device_id_type=pl.DeviceIdType.MESH)
    for f in (across, beside):
        pl.semaphore_signal(barrier, 1, device_id=device(dp, ctx, f), device_id_type=pl.DeviceIdType.MESH)
    own_peak[...] = jnp.full(own_peak.shape, 10.0, jnp.float32)

    def block_of(f):
        return pl.ds(pl.multiple_of(f * rows, rows), rows)

    def y_copy(k):
        return send(
            outgoing.at[k], arriving.at[k], y_send.at[k], y_recv.at[k], device(other_dp, ctx, row)
        )

    def x_copy(k, f):
        part = x_all.at[k, block_of(f)]
        return send(part, part, x_send.at[k], x_recv.at[k], device(dp, ctx, across))

    def c_copy(k, f):
        part = x_all.at[k, block_of(f)]
        return send(part, part, c_send.at[k], c_recv.at[k], device(dp, ctx, beside))

    def r_copy(k, f):
        part = x_all.at[k, block_of(f)]
        return send(part, part, r_send.at[k], r_recv.at[k], device(dp, ctx, beside))

    def columns(k):
        return pl.ds(pl.multiple_of(k * CHUNK, CHUNK), CHUNK)

    def out_copies(k):
        return (
            pltpu.make_async_copy(high_all.at[k], x_high.at[k], out_sem.at[0, k]),
            pltpu.make_async_copy(low_all.at[k], x_low.at[k], out_sem.at[1, k]),
        )

    def fill(k, carry):
        outgoing[k] = grads[other_dp, :, columns(k)].astype(jnp.float32)
        return carry

    def push(k, carry):
        y_copy(k).start()
        return carry

    loads[0].wait()
    lax.fori_loop(0, chunks, fill, 0)
    loads[2].wait()
    own_peak[0 : logit.shape[0], 0 : logit.shape[1]] = logits[...]
    pl.semaphore_wait(barrier, len(same) + 2)
    lax.fori_loop(0, chunks, push, 0)

    def peak_copy(slot, e, d):
        return send(own_peak, peaks.at[slot], pk_send.at[slot], pk_recv.at[slot], shifted(e, d))

    for slot, (e, d) in enumerate(same):
        peak_copy(slot, e, d).start()

    main[...] = jnp.zeros_like(main)
    cross[...] = jnp.zeros_like(cross)

    loads[1].wait()

    def step(s, carry):
        @pl.when(s < chunks)
        def _():
            y_copy(s).wait_recv()
            x_all[s, block_of(row)] = (
                grads[dp, :, columns(s)].astype(jnp.float32) + arriving[s]
            )
            x_copy(s, row).start()
            c_copy(s, row).start()

        @pl.when((s >= 2) & (s < chunks + 2))
        def _():
            k = s - 2
            x_copy(k, across).wait_recv()
            r_copy(k, across).start()

        @pl.when(s >= 3)
        def _():
            k = s - 3
            c_copy(k, beside).wait_recv()
            r_copy(k, diagonal).wait_recv()

            @pl.when(lax.rem(k, JOIN) == JOIN - 1)
            def _():
                head = lax.div(k, JOIN)
                value = jnp.concatenate(
                    [x_all[head * JOIN + i] for i in range(JOIN)], axis=1
                )
                high, low = split(value)
                high_all[head] = high
                low_all[head] = low
                main[...] += dot_nt(high, high)
                cross[...] += dot_nt(high, low)
                for copy in out_copies(head):
                    copy.start()

        return carry

    lax.fori_loop(0, chunks + 3, step, 0)

    def tile(ref, i, j):
        return ref[i * BLOCK : (i + 1) * BLOCK, j * BLOCK : (j + 1) * BLOCK]

    quarter = len(PAIRS) * BLOCK // 4
    for f in range(4):

        @pl.when(row == f)
        def _(f=f):
            for b, (i, j) in enumerate(PAIRS):
                if b * BLOCK < (f + 1) * quarter and (b + 1) * BLOCK > f * quarter:
                    packed[b * BLOCK : (b + 1) * BLOCK] = (
                        tile(main, i, j) + tile(cross, i, j) + tile(cross, j, i).T
                    )

    piece = quarter // n_ctx
    part_rows = piece // cuts

    def piece_of(f, c, h):
        start = (f * n_ctx + c) * piece + h * part_rows
        return pl.ds(pl.multiple_of(start, 8), part_rows)

    def ahead(d):
        return lax.rem(ctx + d, n_ctx)

    def behind(d):
        return lax.rem(ctx + n_ctx - d, n_ctx)

    def rs_copy(h, d):
        n = h * n_ctx + d
        return send(
            packed.at[piece_of(row, ahead(d), h)], partial.at[n],
            rs_send.at[n], rs_recv.at[n], device(dp, ahead(d), row),
        )

    def ag_copy(h, d, c):
        n = h * n_ctx + d
        part = total.at[piece_of(row, c, h)]
        return send(part, part, ag_send.at[n], ag_recv.at[n], device(dp, ahead(d), row))

    def gx_copy(h, d, f):
        n = h * n_ctx + d
        part = total.at[piece_of(f, behind(d), h)]
        return send(part, part, gx_send.at[n], gx_recv.at[n], device(dp, ctx, across))

    def gc_copy(h, d, f):
        n = h * n_ctx + d
        part = total.at[piece_of(f, behind(d), h)]
        return send(part, part, gc_send.at[n], gc_recv.at[n], device(dp, ctx, beside))

    def gr_copy(h, d, f):
        n = h * n_ctx + d
        part = total.at[piece_of(f, behind(d), h)]
        return send(part, part, gr_send.at[n], gr_recv.at[n], device(dp, ctx, beside))

    for h in range(cuts):
        for d in range(1, n_ctx):
            rs_copy(h, d).start()
    for h in range(cuts):
        mine = packed[piece_of(row, ctx, h)]
        for d in range(1, n_ctx):
            rs_copy(h, d).wait_recv()
            mine = mine + partial[h * n_ctx + d]
        total[piece_of(row, ctx, h)] = mine
        for d in range(1, n_ctx):
            ag_copy(h, d, ctx).start()
        gx_copy(h, 0, row).start()
        gc_copy(h, 0, row).start()
    for h in range(cuts):
        for d in range(1, n_ctx):
            ag_copy(h, d, behind(d)).wait_recv()
            gx_copy(h, d, row).start()
            gc_copy(h, d, row).start()
    for h in range(cuts):
        for d in range(n_ctx):
            gx_copy(h, d, across).wait_recv()
            gr_copy(h, d, across).start()

    top = own_peak[...]
    for slot, (e, d) in enumerate(same):
        peak_copy(slot, e, d).wait_recv()
        top = jnp.maximum(top, peaks[slot])
    factor[...] = jnp.sqrt(jnp.minimum(1.0, tau_clip / top))

    for h in range(cuts):
        for d in range(n_ctx):
            gc_copy(h, d, beside).wait_recv()
            gr_copy(h, d, diagonal).wait_recv()

    near = lax.broadcasted_iota(jnp.int32, (BLOCK, BLOCK), 0) == lax.broadcasted_iota(
        jnp.int32, (BLOCK, BLOCK), 1
    )
    diag = jnp.zeros((BLOCK, BLOCK), jnp.float32)
    for b, (i, j) in enumerate(PAIRS):
        if i == j:
            diag = diag + jnp.where(near, total[b * BLOCK : (b + 1) * BLOCK], 0.0)
    trace = jnp.sum(jnp.sum(diag, axis=0, keepdims=True), axis=1, keepdims=True)
    denom = jnp.sqrt(trace) + eps_norm
    squared = denom * denom
    for b, (i, j) in enumerate(PAIRS):
        value = total[b * BLOCK : (b + 1) * BLOCK] / squared
        gram[i * BLOCK : (i + 1) * BLOCK, j * BLOCK : (j + 1) * BLOCK] = value
        if i != j:
            gram[j * BLOCK : (j + 1) * BLOCK, i * BLOCK : (i + 1) * BLOCK] = value.T

    eye = lax.broadcasted_iota(jnp.int32, gram.shape, 0) == lax.broadcasted_iota(
        jnp.int32, gram.shape, 1
    )
    g = gram[...]
    g_parts = split(g)
    poly = ns_b * g + ns_c * product(g_parts, g_parts)
    q0_parts = split(poly + jnp.where(eye, ns_a, 0.0))
    later = product(split(product(g_parts, q0_parts)), q0_parts)
    gram[...] = later
    some = gram[block_of(row)]
    spot = lax.broadcasted_iota(jnp.int32, some.shape, 0) + row * rows == lax.broadcasted_iota(
        jnp.int32, some.shape, 1
    )
    poly = ns_b * some + ns_c * product(split(some), split(later))
    q1 = poly + jnp.where(spot, ns_a, 0.0)
    t = product(split(q1), q0_parts) * (UPDATE_SCALE / denom)
    high, low = split(t)
    t_high[...] = high
    t_low[...] = low

    def last(k, carry):
        y_copy(k).wait_send()
        x_copy(k, row).wait_send()
        c_copy(k, row).wait_send()
        r_copy(k, across).wait_send()
        return carry

    lax.fori_loop(0, chunks, last, 0)
    for head in range(chunks // JOIN):
        for copy in out_copies(head):
            copy.wait()
    for slot, (e, d) in enumerate(same):
        peak_copy(slot, e, d).wait_send()
    for h in range(cuts):
        for d in range(n_ctx):
            if d > 0:
                rs_copy(h, d).wait_send()
                ag_copy(h, d, ctx).wait_send()
            gx_copy(h, d, row).wait_send()
            gc_copy(h, d, row).wait_send()
            gr_copy(h, d, across).wait_send()


def cuts_of(n_ctx):
    piece = len(PAIRS) * BLOCK // (4 * n_ctx)
    return CUTS if piece % (8 * CUTS) == 0 else 1


def gather(grad, logit, n_ctx):
    _, rows, cols = grad.shape
    chunks = cols // CHUNK
    heads = cols // HEAD_COLS
    cuts = cuts_of(n_ctx)
    f32, bf16 = jnp.float32, jnp.bfloat16
    sem = pltpu.SemaphoreType.DMA
    packed_rows = len(PAIRS) * BLOCK
    vmem = pl.BlockSpec(memory_space=pltpu.VMEM)
    anywhere = pl.BlockSpec(memory_space=pl.ANY)
    hbm = pl.BlockSpec(memory_space=pltpu.HBM)
    wide = (heads, KV_RANK, HEAD_COLS)
    return pl.pallas_call(
        functools.partial(gather_kernel, n_ctx, chunks, cuts),
        out_shape=(
            jax.ShapeDtypeStruct(wide, bf16),
            jax.ShapeDtypeStruct(wide, bf16),
            jax.ShapeDtypeStruct((rows, KV_RANK), bf16),
            jax.ShapeDtypeStruct((rows, KV_RANK), bf16),
            jax.ShapeDtypeStruct((8, 128), f32),
        ),
        in_specs=[hbm, hbm],
        out_specs=(anywhere, anywhere, vmem, vmem, vmem),
        scratch_shapes=[
            pltpu.VMEM(logit.shape, f32),
            pltpu.VMEM(grad.shape, bf16),
            pltpu.VMEM((chunks, rows, CHUNK), f32),
            pltpu.VMEM((chunks, rows, CHUNK), f32),
            pltpu.VMEM((chunks, KV_RANK, CHUNK), f32),
            pltpu.VMEM(wide, bf16),
            pltpu.VMEM(wide, bf16),
            pltpu.VMEM((KV_RANK, KV_RANK), f32),
            pltpu.VMEM((KV_RANK, KV_RANK), f32),
            pltpu.VMEM((packed_rows, BLOCK), f32),
            pltpu.VMEM((cuts * n_ctx, packed_rows // (4 * n_ctx * cuts), BLOCK), f32),
            pltpu.VMEM((packed_rows, BLOCK), f32),
            pltpu.VMEM((KV_RANK, KV_RANK), f32),
            pltpu.VMEM((8, 128), f32),
            pltpu.VMEM((2 * n_ctx - 1, 8, 128), f32),
        ]
        + [sem((chunks,))] * 8
        + [sem((2, heads))]
        + [sem((cuts * n_ctx,))] * 10
        + [sem((2 * n_ctx - 1,))] * 2
        + [sem((3,))],
        compiler_params=pltpu.CompilerParams(
            collective_id=0, has_side_effects=True, vmem_limit_bytes=36 * 1024 * 1024
        ),
    )(pltpu.with_memory_space_constraint(grad, pltpu.HBM), pltpu.with_memory_space_constraint(logit, pltpu.HBM))


def apply_kernel(heads, factor, t_high, t_low, x_high, x_low, weight, update, fresh):
    layer = lax.axis_index("dp")
    base = lax.axis_index("ctx") * (heads * pl.num_programs(0)) + pl.program_id(0) * heads
    keep = 1.0 - learn_rate * decay_rate
    for h in range(heads):
        value = product((t_high[...], t_low[...]), (x_high[h], x_low[h]))
        start = h * HEAD_COLS
        update[0, :, start : start + HEAD_COLS] = value
        old = weight[0, :, start : start + HEAD_COLS].astype(jnp.float32)
        moved = old * keep - learn_rate * value
        fresh[0, :, start : start + NOPE] = moved[:, :NOPE] * factor[layer, base + h]
        fresh[0, :, start + NOPE : start + HEAD_COLS] = moved[:, NOPE:]


def apply(factor, t_high, t_low, x_high, x_low, weight, heads):
    chunks = x_high.shape[0]
    rows = weight.shape[1]
    shape = jax.ShapeDtypeStruct(weight.shape, jnp.float32)
    whole = pl.BlockSpec((rows, KV_RANK), lambda i: (0, 0))
    stream = pl.BlockSpec((heads, KV_RANK, HEAD_COLS), lambda i: (i, 0, 0))
    flat = pl.BlockSpec((1, rows, heads * HEAD_COLS), lambda i: (0, 0, i))
    return pl.pallas_call(
        functools.partial(apply_kernel, heads),
        grid=(chunks // heads,),
        out_shape=(shape, shape),
        in_specs=[pl.BlockSpec(memory_space=pltpu.SMEM), whole, whole, stream, stream, flat],
        out_specs=(flat, flat),
        compiler_params=pltpu.CompilerParams(vmem_limit_bytes=20 * 1024 * 1024),
    )(factor, t_high, t_low, x_high, x_low, weight)


def kernel_shards(n_ctx, grad_parts, weight, logit_max):
    x_high, x_low, t_high, t_low, factor = gather(grad_parts[0], logit_max[0, 0], n_ctx)
    return apply(factor, t_high, t_low, x_high, x_low, weight, 4)


def solution(mesh):
    fits = mesh.shape["dp"] == 2 and mesh.shape["fsdp"] == 4 and mesh.shape["ctx"] <= 8
    body = functools.partial(kernel_shards, mesh.shape["ctx"]) if fits else shards
    return jax.shard_map(
        body,
        mesh=mesh,
        in_specs=(P("dp", None, "fsdp", "ctx"), P("dp", "fsdp", "ctx"), P("dp", "ctx", None, None)),
        out_specs=(P("dp", "fsdp", "ctx"), P("dp", "fsdp", "ctx")),
        check_vma=False,
    )
```

```python
import functools
import math

import jax
import jax.numpy as jnp
from jax import lax
from jax.experimental import pallas as pl
from jax.experimental.pallas import tpu as pltpu
from jax.sharding import PartitionSpec as P

KV_RANK = 512
HEADS = 64
NOPE = 128
V_DIM = 128
ITERS = 2


ns_a = 3.4445
ns_b = -4.775
ns_c = 2.0315
eps_norm = 1e-07
tau_clip = 100.0
learn_rate = 0.02
decay_rate = 0.1

HEAD_COLS = NOPE + V_DIM
BLOCK = 128
CHUNK = 256
CUTS = 2
JOIN = HEAD_COLS // CHUNK
SIDE = KV_RANK // BLOCK
PAIRS = [(i, j) for i in range(SIDE) for j in range(i, SIDE)]
UPDATE_SCALE = 0.2 * math.sqrt(max(KV_RANK, HEADS * HEAD_COLS))


def matmul(left, right):
    return jnp.dot(left, right, preferred_element_type=jnp.float32, precision=lax.Precision.HIGHEST)


def gram_sum(block):
    local = matmul(block, block.T)
    half = local.shape[0] // 2
    upper, corner = lax.psum((local[:half], local[half:, half:]), ("ctx", "fsdp"))
    lower = jnp.concatenate([upper[:, half:].T, corner], axis=1)
    return jnp.concatenate([upper, lower], axis=0)


def columns_of(head_factor):
    count = head_factor.shape[0]
    keys = jnp.broadcast_to(head_factor[:, None], (count, NOPE))
    values = jnp.ones((count, V_DIM), dtype=head_factor.dtype)
    return jnp.concatenate([keys, values], axis=1).reshape(-1)


def shards(grad_parts, weight, logit_max):
    parts = grad_parts[0].astype(jnp.float32)
    summed = lax.psum_scatter(parts, "dp", scatter_dimension=0, tiled=True)
    owned = lax.all_to_all(summed[0], "fsdp", split_axis=1, concat_axis=0, tiled=True)
    peak = lax.pmax(logit_max, ("dp", "ctx"))
    gram_raw = gram_sum(owned)
    denom = jnp.sqrt(jnp.trace(gram_raw)) + eps_norm
    iterate = owned / denom
    gram = gram_raw / (denom * denom)
    for step in range(ITERS):
        if step > 0:
            gram = gram_sum(iterate)
        poly = ns_b * gram + ns_c * matmul(gram, gram)
        iterate = ns_a * iterate + matmul(poly, iterate)
    step_value = UPDATE_SCALE * iterate
    back = lax.all_to_all(step_value, "fsdp", split_axis=0, concat_axis=1, tiled=True)
    layer_peak = lax.dynamic_index_in_dim(peak[0, 0], lax.axis_index("dp"), 0, keepdims=False)
    heads_here = HEADS // lax.axis_size("ctx")
    local_peak = lax.dynamic_slice_in_dim(
        layer_peak, lax.axis_index("ctx") * heads_here, heads_here, 0
    )
    factor = jnp.sqrt(jnp.minimum(1.0, tau_clip / local_peak))
    column_factor = columns_of(factor)
    fresh = (
        weight[0].astype(jnp.float32) * (1.0 - learn_rate * decay_rate) - learn_rate * back
    ) * column_factor[None, :]
    return (back[None], fresh[None])


def split(value):
    high = value.astype(jnp.bfloat16)
    low = (value - high.astype(jnp.float32)).astype(jnp.bfloat16)
    return high, low


def dot(left, right):
    return jnp.dot(left, right, preferred_element_type=jnp.float32)


def dot_nt(left, right):
    return lax.dot_general(
        left, right, (((1,), (1,)), ((), ())), preferred_element_type=jnp.float32
    )


def product(left, right):
    (lh, ll), (rh, rl) = left, right
    return dot(lh, rh) + (dot(lh, rl) + dot(ll, rh))


def gather_kernel(
    n_ctx, chunks, cuts,
    grad, logit, x_high, x_low, t_high, t_low, factor,
    logits, grads, outgoing, arriving, x_all, high_all, low_all, main, cross,
    packed, partial, total, gram, own_peak, peaks,
    y_send, y_recv, x_send, x_recv, c_send, c_recv, r_send, r_recv, out_sem,
    rs_send, rs_recv, ag_send, ag_recv, gx_send, gx_recv, gc_send, gc_recv, gr_send, gr_recv,
    pk_send, pk_recv, in_sem,
):
    dp = lax.axis_index("dp")
    ctx = lax.axis_index("ctx")
    row = lax.axis_index("fsdp")
    other_dp = 1 - dp
    across = lax.rem(row + 2, 4)
    beside = row + 1 - 2 * lax.rem(row, 2)
    diagonal = lax.rem(beside + 2, 4)
    rows = grad.shape[1]
    loads = [
        pltpu.make_async_copy(grad.at[layer], grads.at[layer], in_sem.at[i])
        for i, layer in enumerate((other_dp, dp))
    ]
    loads.append(pltpu.make_async_copy(logit, logits, in_sem.at[2]))
    for load in loads:
        load.start()

    def device(d, c, f):
        return {"dp": d, "ctx": c, "fsdp": f}

    def send(src, dst, send_sem, recv_sem, where):
        return pltpu.make_async_remote_copy(
            src_ref=src, dst_ref=dst, send_sem=send_sem, recv_sem=recv_sem,
            device_id=where, device_id_type=pl.DeviceIdType.MESH,
        )

    same = [
        (e, d) for e in range(2) for d in range(n_ctx) if (e, d) != (0, 0)
    ]

    def shifted(e, d):
        return device(lax.rem(dp + e, 2), lax.rem(ctx + d, n_ctx), row)

    barrier = pltpu.get_barrier_semaphore()
    for e, d in same:
        pl.semaphore_signal(barrier, 1, device_id=shifted(e, d), device_id_type=pl.DeviceIdType.MESH)
    for f in (across, beside):
        pl.semaphore_signal(barrier, 1, device_id=device(dp, ctx, f), device_id_type=pl.DeviceIdType.MESH)
    own_peak[...] = jnp.full(own_peak.shape, 10.0, jnp.float32)

    def block_of(f):
        return pl.ds(pl.multiple_of(f * rows, rows), rows)

    def y_copy(k):
        return send(
            outgoing.at[k], arriving.at[k], y_send.at[k], y_recv.at[k], device(other_dp, ctx, row)
        )

    def x_copy(k, f):
        part = x_all.at[k, block_of(f)]
        return send(part, part, x_send.at[k], x_recv.at[k], device(dp, ctx, across))

    def c_copy(k, f):
        part = x_all.at[k, block_of(f)]
        return send(part, part, c_send.at[k], c_recv.at[k], device(dp, ctx, beside))

    def r_copy(k, f):
        part = x_all.at[k, block_of(f)]
        return send(part, part, r_send.at[k], r_recv.at[k], device(dp, ctx, beside))

    def columns(k):
        return pl.ds(pl.multiple_of(k * CHUNK, CHUNK), CHUNK)

    def out_copies(k):
        return (
            pltpu.make_async_copy(high_all.at[k], x_high.at[k], out_sem.at[0, k]),
            pltpu.make_async_copy(low_all.at[k], x_low.at[k], out_sem.at[1, k]),
        )

    def fill(k, carry):
        outgoing[k] = grads[other_dp, :, columns(k)].astype(jnp.float32)
        return carry

    def push(k, carry):
        y_copy(k).start()
        return carry

    loads[0].wait()
    lax.fori_loop(0, chunks, fill, 0)
    loads[2].wait()
    own_peak[0 : logit.shape[0], 0 : logit.shape[1]] = logits[...]
    pl.semaphore_wait(barrier, len(same) + 2)
    lax.fori_loop(0, chunks, push, 0)

    def peak_copy(slot, e, d):
        return send(own_peak, peaks.at[slot], pk_send.at[slot], pk_recv.at[slot], shifted(e, d))

    for slot, (e, d) in enumerate(same):
        peak_copy(slot, e, d).start()

    main[...] = jnp.zeros_like(main)
    cross[...] = jnp.zeros_like(cross)

    loads[1].wait()

    def step(s, carry):
        @pl.when(s < chunks)
        def _():
            y_copy(s).wait_recv()
            x_all[s, block_of(row)] = (
                grads[dp, :, columns(s)].astype(jnp.float32) + arriving[s]
            )
            x_copy(s, row).start()
            c_copy(s, row).start()

        @pl.when((s >= 2) & (s < chunks + 2))
        def _():
            k = s - 2
            x_copy(k, across).wait_recv()
            r_copy(k, across).start()

        @pl.when(s >= 3)
        def _():
            k = s - 3
            c_copy(k, beside).wait_recv()
            r_copy(k, diagonal).wait_recv()

            @pl.when(lax.rem(k, JOIN) == JOIN - 1)
            def _():
                head = lax.div(k, JOIN)
                value = jnp.concatenate(
                    [x_all[head * JOIN + i] for i in range(JOIN)], axis=1
                )
                high, low = split(value)
                high_all[head] = high
                low_all[head] = low
                main[...] += dot_nt(high, high)
                cross[...] += dot_nt(high, low)
                for copy in out_copies(head):
                    copy.start()

        return carry

    lax.fori_loop(0, chunks + 3, step, 0)

    def tile(ref, i, j):
        return ref[i * BLOCK : (i + 1) * BLOCK, j * BLOCK : (j + 1) * BLOCK]

    quarter = len(PAIRS) * BLOCK // 4
    for f in range(4):

        @pl.when(row == f)
        def _(f=f):
            for b, (i, j) in enumerate(PAIRS):
                if b * BLOCK < (f + 1) * quarter and (b + 1) * BLOCK > f * quarter:
                    packed[b * BLOCK : (b + 1) * BLOCK] = (
                        tile(main, i, j) + tile(cross, i, j) + tile(cross, j, i).T
                    )

    piece = quarter // n_ctx
    part_rows = piece // cuts

    def piece_of(f, c, h):
        start = (f * n_ctx + c) * piece + h * part_rows
        return pl.ds(pl.multiple_of(start, 8), part_rows)

    def ahead(d):
        return lax.rem(ctx + d, n_ctx)

    def behind(d):
        return lax.rem(ctx + n_ctx - d, n_ctx)

    def rs_copy(h, d):
        n = h * n_ctx + d
        return send(
            packed.at[piece_of(row, ahead(d), h)], partial.at[n],
            rs_send.at[n], rs_recv.at[n], device(dp, ahead(d), row),
        )

    def ag_copy(h, d, c):
        n = h * n_ctx + d
        part = total.at[piece_of(row, c, h)]
        return send(part, part, ag_send.at[n], ag_recv.at[n], device(dp, ahead(d), row))

    def gx_copy(h, d, f):
        n = h * n_ctx + d
        part = total.at[piece_of(f, behind(d), h)]
        return send(part, part, gx_send.at[n], gx_recv.at[n], device(dp, ctx, across))

    def gc_copy(h, d, f):
        n = h * n_ctx + d
        part = total.at[piece_of(f, behind(d), h)]
        return send(part, part, gc_send.at[n], gc_recv.at[n], device(dp, ctx, beside))

    def gr_copy(h, d, f):
        n = h * n_ctx + d
        part = total.at[piece_of(f, behind(d), h)]
        return send(part, part, gr_send.at[n], gr_recv.at[n], device(dp, ctx, beside))

    for h in range(cuts):
        for d in range(1, n_ctx):
            rs_copy(h, d).start()
    for h in range(cuts):
        mine = packed[piece_of(row, ctx, h)]
        for d in range(1, n_ctx):
            rs_copy(h, d).wait_recv()
            mine = mine + partial[h * n_ctx + d]
        total[piece_of(row, ctx, h)] = mine
        for d in range(1, n_ctx):
            ag_copy(h, d, ctx).start()
        gx_copy(h, 0, row).start()
        gc_copy(h, 0, row).start()
    for h in range(cuts):
        for d in range(1, n_ctx):
            ag_copy(h, d, behind(d)).wait_recv()
            gx_copy(h, d, row).start()
            gc_copy(h, d, row).start()
    for h in range(cuts):
        for d in range(n_ctx):
            gx_copy(h, d, across).wait_recv()
            gr_copy(h, d, across).start()

    top = own_peak[...]
    for slot, (e, d) in enumerate(same):
        peak_copy(slot, e, d).wait_recv()
        top = jnp.maximum(top, peaks[slot])
    factor[...] = jnp.sqrt(jnp.minimum(1.0, tau_clip / top))

    for h in range(cuts):
        for d in range(n_ctx):
            gc_copy(h, d, beside).wait_recv()
            gr_copy(h, d, diagonal).wait_recv()

    near = lax.broadcasted_iota(jnp.int32, (BLOCK, BLOCK), 0) == lax.broadcasted_iota(
        jnp.int32, (BLOCK, BLOCK), 1
    )
    diag = jnp.zeros((BLOCK, BLOCK), jnp.float32)
    for b, (i, j) in enumerate(PAIRS):
        if i == j:
            diag = diag + jnp.where(near, total[b * BLOCK : (b + 1) * BLOCK], 0.0)
    trace = jnp.sum(jnp.sum(diag, axis=0, keepdims=True), axis=1, keepdims=True)
    denom = jnp.sqrt(trace) + eps_norm
    squared = denom * denom
    for b, (i, j) in enumerate(PAIRS):
        value = total[b * BLOCK : (b + 1) * BLOCK] / squared
        gram[i * BLOCK : (i + 1) * BLOCK, j * BLOCK : (j + 1) * BLOCK] = value
        if i != j:
            gram[j * BLOCK : (j + 1) * BLOCK, i * BLOCK : (i + 1) * BLOCK] = value.T

    eye = lax.broadcasted_iota(jnp.int32, gram.shape, 0) == lax.broadcasted_iota(
        jnp.int32, gram.shape, 1
    )
    g = gram[...]
    g_parts = split(g)
    poly = ns_b * g + ns_c * product(g_parts, g_parts)
    q0_parts = split(poly + jnp.where(eye, ns_a, 0.0))
    later = product(split(product(g_parts, q0_parts)), q0_parts)
    gram[...] = later
    some = gram[block_of(row)]
    spot = lax.broadcasted_iota(jnp.int32, some.shape, 0) + row * rows == lax.broadcasted_iota(
        jnp.int32, some.shape, 1
    )
    poly = ns_b * some + ns_c * product(split(some), split(later))
    q1 = poly + jnp.where(spot, ns_a, 0.0)
    t = product(split(q1), q0_parts) * (UPDATE_SCALE / denom)
    high, low = split(t)
    t_high[...] = high
    t_low[...] = low

    def last(k, carry):
        y_copy(k).wait_send()
        x_copy(k, row).wait_send()
        c_copy(k, row).wait_send()
        r_copy(k, across).wait_send()
        return carry

    lax.fori_loop(0, chunks, last, 0)
    for head in range(chunks // JOIN):
        for copy in out_copies(head):
            copy.wait()
    for slot, (e, d) in enumerate(same):
        peak_copy(slot, e, d).wait_send()
    for h in range(cuts):
        for d in range(n_ctx):
            if d > 0:
                rs_copy(h, d).wait_send()
                ag_copy(h, d, ctx).wait_send()
            gx_copy(h, d, row).wait_send()
            gc_copy(h, d, row).wait_send()
            gr_copy(h, d, across).wait_send()


def cuts_of(n_ctx):
    piece = len(PAIRS) * BLOCK // (4 * n_ctx)
    return CUTS if piece % (8 * CUTS) == 0 else 1


def gather(grad, logit, n_ctx):
    _, rows, cols = grad.shape
    chunks = cols // CHUNK
    heads = cols // HEAD_COLS
    cuts = cuts_of(n_ctx)
    f32, bf16 = jnp.float32, jnp.bfloat16
    sem = pltpu.SemaphoreType.DMA
    packed_rows = len(PAIRS) * BLOCK
    vmem = pl.BlockSpec(memory_space=pltpu.VMEM)
    anywhere = pl.BlockSpec(memory_space=pl.ANY)
    hbm = pl.BlockSpec(memory_space=pltpu.HBM)
    wide = (heads, KV_RANK, HEAD_COLS)
    return pl.pallas_call(
        functools.partial(gather_kernel, n_ctx, chunks, cuts),
        out_shape=(
            jax.ShapeDtypeStruct(wide, bf16),
            jax.ShapeDtypeStruct(wide, bf16),
            jax.ShapeDtypeStruct((rows, KV_RANK), bf16),
            jax.ShapeDtypeStruct((rows, KV_RANK), bf16),
            jax.ShapeDtypeStruct((8, 128), f32),
        ),
        in_specs=[hbm, hbm],
        out_specs=(anywhere, anywhere, vmem, vmem, vmem),
        scratch_shapes=[
            pltpu.VMEM(logit.shape, f32),
            pltpu.VMEM(grad.shape, bf16),
            pltpu.VMEM((chunks, rows, CHUNK), f32),
            pltpu.VMEM((chunks, rows, CHUNK), f32),
            pltpu.VMEM((chunks, KV_RANK, CHUNK), f32),
            pltpu.VMEM(wide, bf16),
            pltpu.VMEM(wide, bf16),
            pltpu.VMEM((KV_RANK, KV_RANK), f32),
            pltpu.VMEM((KV_RANK, KV_RANK), f32),
            pltpu.VMEM((packed_rows, BLOCK), f32),
            pltpu.VMEM((cuts * n_ctx, packed_rows // (4 * n_ctx * cuts), BLOCK), f32),
            pltpu.VMEM((packed_rows, BLOCK), f32),
            pltpu.VMEM((KV_RANK, KV_RANK), f32),
            pltpu.VMEM((8, 128), f32),
            pltpu.VMEM((2 * n_ctx - 1, 8, 128), f32),
        ]
        + [sem((chunks,))] * 8
        + [sem((2, heads))]
        + [sem((cuts * n_ctx,))] * 10
        + [sem((2 * n_ctx - 1,))] * 2
        + [sem((3,))],
        compiler_params=pltpu.CompilerParams(
            collective_id=0, has_side_effects=True, vmem_limit_bytes=36 * 1024 * 1024
        ),
    )(pltpu.with_memory_space_constraint(grad, pltpu.HBM), pltpu.with_memory_space_constraint(logit, pltpu.HBM))


def apply_kernel(heads, factor, t_high, t_low, x_high, x_low, weight, update, fresh):
    layer = lax.axis_index("dp")
    base = lax.axis_index("ctx") * (heads * pl.num_programs(0)) + pl.program_id(0) * heads
    keep = 1.0 - learn_rate * decay_rate
    for h in range(heads):
        value = product((t_high[...], t_low[...]), (x_high[h], x_low[h]))
        start = h * HEAD_COLS
        update[0, :, start : start + HEAD_COLS] = value
        old = weight[0, :, start : start + HEAD_COLS].astype(jnp.float32)
        moved = old * keep - learn_rate * value
        fresh[0, :, start : start + NOPE] = moved[:, :NOPE] * factor[layer, base + h]
        fresh[0, :, start + NOPE : start + HEAD_COLS] = moved[:, NOPE:]


def apply(factor, t_high, t_low, x_high, x_low, weight, heads):
    chunks = x_high.shape[0]
    rows = weight.shape[1]
    shape = jax.ShapeDtypeStruct(weight.shape, jnp.float32)
    whole = pl.BlockSpec((rows, KV_RANK), lambda i: (0, 0))
    stream = pl.BlockSpec((heads, KV_RANK, HEAD_COLS), lambda i: (i, 0, 0))
    flat = pl.BlockSpec((1, rows, heads * HEAD_COLS), lambda i: (0, 0, i))
    return pl.pallas_call(
        functools.partial(apply_kernel, heads),
        grid=(chunks // heads,),
        out_shape=(shape, shape),
        in_specs=[pl.BlockSpec(memory_space=pltpu.SMEM), whole, whole, stream, stream, flat],
        out_specs=(flat, flat),
        compiler_params=pltpu.CompilerParams(vmem_limit_bytes=20 * 1024 * 1024),
    )(factor, t_high, t_low, x_high, x_low, weight)


def kernel_shards(n_ctx, grad_parts, weight, logit_max):
    x_high, x_low, t_high, t_low, factor = gather(grad_parts[0], logit_max[0, 0], n_ctx)
    return apply(factor, t_high, t_low, x_high, x_low, weight, 4)


def solution(mesh):
    fits = mesh.shape["dp"] == 2 and mesh.shape["fsdp"] == 4 and mesh.shape["ctx"] <= 8
    body = functools.partial(kernel_shards, mesh.shape["ctx"]) if fits else shards
    return jax.shard_map(
        body,
        mesh=mesh,
        in_specs=(P("dp", None, "fsdp", "ctx"), P("dp", "fsdp", "ctx"), P("dp", "ctx", None, None)),
        out_specs=(P("dp", "fsdp", "ctx"), P("dp", "fsdp", "ctx")),
        check_vma=False,
    )
```
